256 devices in a mesh: rep: 16 (over x, y), mem: 16 (over z, core).
Axes of the slice: x: 4, y: 4, z: 8, core: 2. Of those that a mesh axis runs over, the one named last changes fastest.
Arguments:
- schur_blocks: bfloat16 [512, 1024, 1024], P(('rep', 'mem')), as said below
- rigid_modes: float32 [512, 6, 1024], P(('rep', 'mem')), may hold values from -0.25 to 0.25
- coarse_inverse: float32 [768, 768], P(None, 'mem'), as said below
- coarse_rhs: float32 [16, 768], P(None, 'mem'), may hold values from -18 to 18
- subdomain_rhs: float32 [16, 512, 1024], P(None, ('rep', 'mem'))
- partner: int32 [512, 8], P(('rep', 'mem')), may hold values from 0 to 4095, as said below
- cluster_of: int32 [512], P(('rep', 'mem')), may hold values from 0 to 127, as said below
Outputs:
- multipliers: float32 [16, 512, 1024], P(None, ('rep', 'mem'))
- projected: float32 [16, 512, 1024], P(None, ('rep', 'mem'))
The draws below stay inside these ranges and needn't reach their ends.
Inputs may be any that keep to these rules, and one draw needn't show every extreme that they name: partner pairs slots: partner[partner[i]] = i and partner[i] != i over the flattened slots i = 8 * s + j. A slot's partner lies on a device with the same rep index whose mem index equals its own or differs from it in exactly one bit. Two different devices share at most 4 paired slots, and in every rep group some two devices share exactly 4. `cluster_of`: each cluster holds exactly 4 subdomains. `schur_blocks`: each subdomain's block is symmetric. `coarse_inverse`: Symmetric.
All inputs are finite; a program needn't handle non-finite values.
Results may differ from the reference program's by a relative error of at most 0.0003.
Values sent between devices are 32-bit elements; how exact they have to be, the bound alone decides.
A program may use at most 64 MiB of HBM per device.

```python
import math
import jax
import jax.numpy as jnp
from jax import lax

NLAM = 1024
BW = 128
BLK = 8
MODES = 6
CASES = 16
SUB_DEV = 2
SUB_PER_CL = 4
ITERS = 2
SUBS = 512
CLUSTERS = 128
COARSE = 768
N_REP = 16
N_MEM = 16


def symmetric_block(key, order, lo_diag, hi_diag, spread_scale):
    key_off, key_diag = jax.random.split(key)
    noise = jax.random.normal(key_off, (order, order), jnp.float32)
    diagonal = jax.random.uniform(key_diag, (order,), jnp.float32, lo_diag, hi_diag)
    identity = jnp.eye(order, dtype=jnp.float32)
    symmetric = (noise + noise.T) * (spread_scale / math.sqrt(2.0))
    return symmetric * (1.0 - identity) + identity * diagonal[None, :]


def draw_schur_blocks(key, part):
    spread_scale = 0.38 / math.sqrt(NLAM)

    def single(index):
        return symmetric_block(jax.random.fold_in(key, index), NLAM, 1.0, 2.5, spread_scale).astype(jnp.bfloat16)
    return lax.map(single, jnp.arange(SUBS, dtype=jnp.int32))


def draw_coarse_inverse(key, part):
    return symmetric_block(key, COARSE, 1.0, 2.0, 0.35 / math.sqrt(COARSE))


def draw_subdomain_rhs(key, part):
    key_main, key_sub, key_case = jax.random.split(key, 3)
    ramp_base = jnp.arange(SUBS, dtype=jnp.float32) / float(max(SUBS - 1, 1))
    sub_scale = jnp.exp(jax.random.uniform(key_sub, (1, SUBS, 1), jnp.float32, math.log(0.25), math.log(2.5)))
    case_scale = jnp.exp(jax.random.uniform(key_case, (CASES, 1, 1), jnp.float32, math.log(0.25), math.log(2.5)))
    noise = jax.random.normal(key_main, (CASES, SUBS, NLAM), jnp.float32)
    ramp_line = 0.5 + ramp_base
    return noise * sub_scale * case_scale * ramp_line[None, :, None]


def draw_partner(key, part):
    slot_count = SUB_DEV * BLK
    dev_total = N_REP * N_MEM
    bit_count = int(N_MEM).bit_length() - 1
    capacity = slot_count // 4
    key_count, key_top, key_order = jax.random.split(key, 3)
    device = jnp.arange(dev_total, dtype=jnp.int32)
    member = device % N_MEM
    group_index = device // N_MEM
    bit_range = jnp.arange(bit_count, dtype=jnp.int32)
    bit_values = jnp.left_shift(jnp.ones((bit_count,), jnp.int32), bit_range)
    halves = jax.random.randint(key_count, (dev_total, bit_count), 0, capacity // 2 + 1, dtype=jnp.int32) * 2
    lowest = device[:, None] - jnp.bitwise_and(member[:, None], bit_values[None, :])
    counts = halves[lowest, bit_range[None, :]]
    chosen = jax.random.randint(key_top, (N_REP,), 0, N_MEM, dtype=jnp.int32)
    forced = member // 2 == chosen[group_index] // 2
    counts = counts.at[:, 0].set(jnp.where(forced, capacity, counts[:, 0]))
    seg_ends = jnp.cumsum(counts, axis=1)
    seg_starts = seg_ends - counts
    remote = seg_ends[:, bit_count - 1]
    rest_count = slot_count - remote
    score_top = (1 << 30) // slot_count
    scores = jax.random.randint(key_order, (dev_total, slot_count), 0, score_top, dtype=jnp.int32) * slot_count
    scores = scores + jnp.arange(slot_count, dtype=jnp.int32)[None, :]
    slot_order = jnp.argsort(scores, axis=1).astype(jnp.int32)
    position = jnp.arange(slot_count, dtype=jnp.int32)[None, :]
    segment = jnp.sum((position[:, :, None] >= seg_ends[:, None, :]).astype(jnp.int32), axis=2)
    segment = jnp.minimum(segment, bit_count - 1)
    seg_begin = jnp.take_along_axis(seg_starts, segment, axis=1)
    offset = position - seg_begin
    peer_dev = jnp.bitwise_xor(device[:, None], jnp.left_shift(jnp.ones_like(segment), segment))
    peer_pos = jnp.clip(seg_starts[peer_dev, segment] + offset, 0, slot_count - 1)
    remote_value = peer_dev * slot_count + slot_order[peer_dev, peer_pos]
    half_rest = rest_count // 2
    inner_pos = position - remote[:, None]
    mate_pos = remote[:, None] + jnp.mod(inner_pos + half_rest[:, None], jnp.maximum(rest_count, 1)[:, None])
    mate_pos = jnp.clip(mate_pos, 0, slot_count - 1)
    local_value = device[:, None] * slot_count + jnp.take_along_axis(slot_order, mate_pos, axis=1)
    pair_value = jnp.where(position < remote[:, None], remote_value, local_value)
    inverse = jnp.argsort(slot_order, axis=1).astype(jnp.int32)
    result = jnp.take_along_axis(pair_value, inverse, axis=1)
    return result.reshape(dev_total * SUB_DEV, BLK).astype(jnp.int32)


def draw_cluster_of(key, part):
    score_top = (1 << 30) // SUBS
    scores = jax.random.randint(key, (SUBS,), 0, score_top, dtype=jnp.int32) * SUBS + jnp.arange(SUBS, dtype=jnp.int32)
    ranking = jnp.argsort(scores).astype(jnp.int32)
    return (ranking // SUB_PER_CL).astype(jnp.int32)


def steps_of(stream_key, shape, cuts, smallest, high):
    def one(axis_at, parts):
        draws = jax.random.uniform(jax.random.fold_in(jax.random.fold_in(stream_key, 6), axis_at), (parts,), jnp.float32, smallest / len(cuts), high / len(cuts))
        return jnp.repeat(jnp.exp(draws), shape[axis_at] // parts).reshape((-1,) + (1,) * (len(shape) - axis_at - 1))

    loudness = one(*cuts[0])
    for cut in cuts[1:]:
        loudness = loudness * one(*cut)
    return loudness


def centred(key, shape, deviation, most, cuts=(), held_as=jnp.bfloat16):
    drawn = deviation * jax.random.normal(key, shape, jnp.float32)
    if cuts:
        drawn = drawn * steps_of(key, shape, cuts, -0.22, 0.18)
    return jnp.clip(drawn, -most, most).astype(held_as)


def setup_inputs(seed: int = 0) -> dict:
    key_list = jax.random.split(jax.random.key(seed), 8)
    schur_blocks = draw_schur_blocks(jax.random.fold_in(key_list[7], 71), 0)
    rigid_modes = centred(key_list[1], (SUBS, MODES, NLAM), (2.5 / (NLAM * SUB_PER_CL) ** 0.5), 0.25, ((0, 256),), jnp.float32)
    coarse_inverse = draw_coarse_inverse(jax.random.fold_in(key_list[7], 71), 0)
    coarse_rhs = centred(key_list[3], (CASES, COARSE), 3.0, 18.0, ((1, 16),), jnp.float32)
    subdomain_rhs = draw_subdomain_rhs(jax.random.fold_in(key_list[7], 71), 0)
    partner = draw_partner(jax.random.fold_in(key_list[7], 71), 0)
    cluster_of = draw_cluster_of(jax.random.fold_in(key_list[7], 71), 0)
    return {"schur_blocks": schur_blocks, "rigid_modes": rigid_modes, "coarse_inverse": coarse_inverse, "coarse_rhs": coarse_rhs, "subdomain_rhs": subdomain_rhs, "partner": partner, "cluster_of": cluster_of}


precise = lax.Precision.HIGHEST


def assemble(contributions, signs, partner_flat):
    row_count = contributions.shape[0]
    signed = contributions.reshape(row_count, SUBS * BLK, BW) * signs[None, :, None]
    joined = signed + jnp.take(signed, partner_flat, axis=1)
    return joined.reshape(row_count, SUBS, NLAM)


def schur_apply(schur_blocks, vector, sign_rows, signs, partner_flat):
    flipped = (vector * sign_rows[None]).astype(jnp.bfloat16)

    def single(pair_args):
        matrix, column = pair_args
        return jnp.einsum("ij,cj->ci", matrix.astype(jnp.float32), column.astype(jnp.float32), precision=precise)

    local_terms = lax.map(single, (schur_blocks, jnp.swapaxes(flipped, 0, 1)))
    return assemble(jnp.swapaxes(local_terms, 0, 1), signs, partner_flat)


def coarse_terms(rigid_modes, sign_rows, cluster_of, vector):
    partials = jnp.einsum("smj,csj->scm", rigid_modes, vector * sign_rows[None], precision=precise)
    summed = jax.ops.segment_sum(partials, cluster_of, num_segments=CLUSTERS)
    return jnp.transpose(summed, (1, 0, 2)).reshape(CASES, COARSE)


def coarse_solve(coarse_inverse, coarse_vec):
    return jnp.einsum("ab,cb->ca", coarse_inverse, coarse_vec, precision=precise)


def spread_terms(rigid_modes, cluster_of, solution):
    per_cluster = solution.reshape(solution.shape[0], CLUSTERS, MODES)
    own_rows = jnp.take(per_cluster, cluster_of, axis=1)
    return jnp.einsum("smj,csm->csj", rigid_modes, own_rows, precision=precise)


def inner_sum(first, second):
    return 0.5 * jnp.sum(first * second, axis=(1, 2))


def reference(schur_blocks, rigid_modes, coarse_inverse, coarse_rhs, subdomain_rhs, partner, cluster_of):
    partner_flat = partner.reshape(SUBS * BLK).astype(jnp.int32)
    slot_ids = jnp.arange(SUBS * BLK, dtype=jnp.int32)
    signs = jnp.where(slot_ids < partner_flat, 1.0, -1.0).astype(jnp.float32)
    sign_rows = jnp.repeat(signs.reshape(SUBS, BLK), BW, axis=1)

    def project(vector):
        solution = coarse_solve(coarse_inverse, coarse_terms(rigid_modes, sign_rows, cluster_of, vector))
        return vector - assemble(spread_terms(rigid_modes, cluster_of, solution), signs, partner_flat)

    dual_rhs = assemble(subdomain_rhs, signs, partner_flat)
    multipliers = assemble(spread_terms(rigid_modes, cluster_of, coarse_solve(coarse_inverse, coarse_rhs)), signs, partner_flat)
    residual = dual_rhs - schur_apply(schur_blocks, multipliers, sign_rows, signs, partner_flat)
    projected = project(residual)
    norm_now = inner_sum(projected, projected)
    direction = projected
    for iteration in range(ITERS):
        curved = schur_apply(schur_blocks, direction, sign_rows, signs, partner_flat)
        step_size = norm_now / inner_sum(direction, curved)
        multipliers = multipliers + step_size[:, None, None] * direction
        residual = residual - step_size[:, None, None] * curved
        projected = project(residual)
        norm_next = inner_sum(projected, projected)
        direction = projected + (norm_next / norm_now)[:, None, None] * direction
        norm_now = norm_next
    return multipliers, projected
```

```python
import functools

import jax
import jax.numpy as jnp
from jax import lax
from jax.experimental import pallas as pl
from jax.experimental.pallas import tpu as pltpu
from jax.sharding import PartitionSpec as P

MESH = pl.DeviceIdType.MESH
F32 = jnp.float32
BF = jnp.bfloat16
CASES = 16
MODES = 6
SLOTS = 16
LANES = 128
ENT = 144
STEPS = 3


def split3(x):
    hi = x.astype(BF)
    rest = x - hi.astype(F32)
    mid = rest.astype(BF)
    low = (rest - mid.astype(F32)).astype(BF)
    return hi, mid, low


def mm(a, b, nt=False):
    return lax.dot_general(
        a, b, (((1,), (1 if nt else 0,)), ((), ())), preferred_element_type=F32
    )


def dot3(x, w, nt=False):
    n = x.shape[0]
    a = jnp.concatenate(split3(x), axis=0)
    r1 = mm(a, w[0], nt)
    r2 = mm(a[: 2 * n], w[1], nt)
    r3 = mm(a[:n], w[2], nt)
    return r1[:n] + ((r1[n : 2 * n] + r2[:n]) + (r1[2 * n :] + r2[n:] + r3))


def dot_exact(x, onehot, nt=False):
    n = x.shape[0]
    r = mm(jnp.concatenate(split3(x), axis=0), onehot, nt)
    return r[:n] + (r[n : 2 * n] + r[2 * n :])


def total16(ref, *lead):
    parts = [ref[(*lead, i)] for i in range(16)]
    while len(parts) > 1:
        parts = [a + b for a, b in zip(parts[::2], parts[1::2])]
    return parts[0]


def kernel(
    n_rep, n_mem,
    partner_ref, cluster_ref, modes_ref, qinv_ref, crhs_ref, rhs_ref, schur_hbm,
    out_l, out_p,
    kbuf, wt, qpad, qp, qn, sc, scy,
    gall, gown, gsend, tall0, tall1, tall2, town, tsend,
    crpad, crall, yall, eb, rs, ra, gb,
    tm, tr,
    lam, p0, p1, d1,
    key, code, pos, sslot, sgn,
    ksem, send, recv,
):
    rep = lax.axis_index("rep")
    mem = lax.axis_index("mem")
    kcopy = pltpu.make_async_copy(schur_hbm, kbuf, ksem)
    kcopy.start()
    bar = pltpu.get_barrier_semaphore()

    def greet(axis, me, n):
        def body(off, _):
            pl.semaphore_signal(
                bar, inc=1, device_id={axis: me ^ off}, device_id_type=MESH
            )
            return 0
        lax.fori_loop(1, n, body, 0)

    greet("mem", mem, n_mem)
    greet("rep", rep, n_rep)

    def remote(src, dst, r, axis, peer):
        return pltpu.make_async_remote_copy(
            src_ref=src, dst_ref=dst, send_sem=send.at[r], recv_sem=recv.at[r],
            device_id={axis: peer}, device_id_type=MESH,
        )

    def scatter(src_of, dst, r, axis, me, n):
        def body(off, _):
            peer = me ^ off
            remote(src_of(peer), dst.at[me], r, axis, peer).start()
            return 0
        lax.fori_loop(1, n, body, 0)

    def finish(dst, r, axis, me, n):
        most = dst.at[pl.ds(0, n - 1)]
        copy = remote(most, most, r, axis, me ^ 1)
        copy.wait_recv()
        return copy

    def exchange_start(src, dst, r):
        for bit in range(4):
            remote(
                src.at[pl.ds(4 * bit, 4)], dst.at[pl.ds(SLOTS + 4 * bit, 4)],
                r, "mem", mem ^ (1 << bit),
            ).start()

    def exchange_wait(src, dst, r):
        copy = remote(src, dst.at[pl.ds(SLOTS, SLOTS)], r, "mem", mem ^ 1)
        copy.wait_recv()
        return copy

    for i in range(SLOTS):
        value = partner_ref[i // 8, i % 8]
        key[i] = value & (16 * n_mem - 1)
        first = (rep * n_mem + mem) * SLOTS + i < value
        sgn[i] = jnp.where(first, 1.0, -1.0).astype(F32)

    def table(i, _):
        mine = key[i]
        base = mine & ~15
        sent = jnp.int32(0)
        got = jnp.int32(0)
        for k in range(SLOTS):
            other = key[k]
            same = (other & ~15) == base
            sent += jnp.where(jnp.logical_and(same, other < mine), 1, 0)
            got += jnp.where(jnp.logical_and(same, i > k), 1, 0)
        diff = (mine >> 4) ^ mem
        bit = (
            jnp.where(diff >= 2, 4, 0) + jnp.where(diff >= 4, 4, 0)
            + jnp.where(diff >= 8, 4, 0)
        )
        here = diff == 0
        code[i] = jnp.where(here, -1, bit + sent)
        pos[i] = jnp.where(here, mine & 15, SLOTS + bit + (got & 3))
        return 0
    lax.fori_loop(0, SLOTS, table, 0)

    def places(p, _):
        found = jnp.int32(0)
        for k in range(SLOTS):
            found += jnp.where(code[k] == p, k, 0)
        sslot[p] = found & 15
        return 0
    lax.fori_loop(0, SLOTS, places, 0)

    for i in range(SLOTS):
        s, j = divmod(i, 8)
        for own in (gown, gall):
            own[i, 0:MODES, :] = modes_ref[s, :, LANES * j : LANES * (j + 1)]
            own[i, MODES:8, :] = jnp.full((2, LANES), cluster_ref[s].astype(F32), F32)
    for p in range(SLOTS):
        gsend[p] = gown[sslot[p]]

    odd = (mem & 1) == 1
    crpad[...] = jnp.zeros_like(crpad)
    crpad[:, 0:48] = crhs_ref[...]
    place = crpad[...]
    crall[mem] = jnp.where(odd, pltpu.roll(place, 64, 1), place)

    pl.semaphore_wait(bar, n_mem + n_rep - 2)

    pending = []
    scatter(lambda peer: crall.at[mem], crall, 0, "mem", mem, n_mem)
    exchange_start(gsend, gall, 1)

    qpad[...] = jnp.zeros_like(qpad)
    qpad[:, 0:48] = qinv_ref[...]
    place = qpad[...]
    qpad[...] = jnp.where(odd, pltpu.roll(place, 64, 1), place)
    qn[...] = jnp.zeros_like(qn)
    for m in range(16):
        parts = split3(qpad[48 * m : 48 * (m + 1), :])
        for t in range(3):
            qn[t, 64 * m : 64 * m + 48, :] = parts[t]
    for m in range(MODES):
        parts = split3(qpad[pl.ds(m, LANES, stride=MODES), :])
        for t in range(3):
            qp[t, LANES * m : LANES * (m + 1), :] = parts[t]
    wt[...] = jnp.zeros_like(wt)

    row = lax.broadcasted_iota(jnp.int32, (8, LANES), 0)
    blank = jnp.zeros((8, LANES), F32)

    def store_modes(i, half, first_row, tile):
        tile = jnp.where(row < MODES, tile, 0.0)
        both = [blank, tile] if half else [tile, blank]
        parts = split3(jnp.concatenate(both, axis=0))
        for t in range(3):
            wt[t, first_row : first_row + 16, LANES * i : LANES * (i + 1)] = parts[t]

    for i in range(SLOTS):
        store_modes(i, i // 8, 128, gown[i])

    pending.append(exchange_wait(gsend, gall, 1))
    ids = []
    for i in range(SLOTS):
        got = gall[pos[i]]
        store_modes(i, i % 2, 16 * (i // 2), -got)
        ids.append(jnp.broadcast_to(got[MODES : MODES + 1, :], (8, LANES)))
    for s in range(2):
        ids.append(jnp.full((8, LANES), cluster_ref[s].astype(F32), F32))

    lane = lax.broadcasted_iota(jnp.int32, (16, LANES), 1)
    mode = lax.broadcasted_iota(jnp.int32, (16, LANES), 0) & 7
    lane_f = lane.astype(F32)
    in_half = lane & 63
    sub = (in_half * 43) >> 8
    sub_mode = in_half - MODES * sub
    fits = jnp.logical_and(in_half < 48, sub_mode == mode)
    first_cluster = (sub + 8 * (lane >> 6)).astype(F32)
    for a in range(9):
        pair = jnp.concatenate([ids[2 * a], ids[2 * a + 1]], axis=0)
        rows = slice(16 * a, 16 * (a + 1))
        for m in range(MODES):
            hit = jnp.logical_and(mode == m, lane_f == pair)
            sc[rows, LANES * m : LANES * (m + 1)] = jnp.where(hit, 1.0, 0.0).astype(BF)
        for j in range(8):
            hit = jnp.logical_and(fits, first_cluster + 16.0 * j == pair)
            scy[rows, LANES * j : LANES * (j + 1)] = jnp.where(hit, 1.0, 0.0).astype(BF)

    def pairs(ref):
        return jnp.concatenate(
            [ref[2 * j] + ref[2 * j + 1] for j in range(8)], axis=1
        )

    def spread(y_slice, step):
        y = yall.at[step]
        r = 2 + step
        y[mem] = y_slice
        scatter(lambda peer: y.at[mem], y, r, "mem", mem, n_mem)
        pending.append(finish(y, r, "mem", mem, n_mem))
        picked = dot_exact(pairs(y), scy[...], nt=True)
        return dot3(picked, (wt[0], wt[1], wt[2]))

    def schur(src):
        out = []
        for s in range(2):
            flat = jnp.concatenate(
                [src[8 * s + j].astype(BF) for j in range(8)], axis=1
            )
            out.append(mm(flat, kbuf[s]))
        return out

    def lanes_of(values, i):
        return values[:, LANES * i : LANES * (i + 1)]

    def reduce_start(step, scalars):
        t = (tall0, tall1, tall2)[step]
        e = eb.at[step]
        base = 6 + 4 * step
        for i in range(SLOTS):
            t[i] = town[step, i]
        flat = jnp.concatenate([town[step, i] for i in range(SLOTS)], axis=1)
        own = dot3(flat, (wt[0], wt[1], wt[2]), nt=True)
        dense = dot_exact(own, sc[...])
        for m in range(MODES):
            e[:, m, :] = lanes_of(dense, m)
        for k, value in enumerate(scalars):
            e[:, MODES + k, :] = value
        rs[step, mem] = e[mem]
        scatter(lambda peer: e.at[peer], rs.at[step], base, "mem", mem, n_mem)
        for p in range(SLOTS):
            tsend[step, p] = town[step, sslot[p]]
        exchange_start(tsend.at[step], t, base + 1)
        pending.append(finish(rs.at[step], base, "mem", mem, n_mem))
        ra[step, rep] = total16(rs, step)
        scatter(lambda peer: ra.at[step, rep], ra.at[step], base + 2, "rep", rep, n_rep)
        pending.append(finish(ra.at[step], base + 2, "rep", rep, n_rep))
        g = gb.at[step]
        g[mem] = total16(ra, step)
        scatter(lambda peer: g.at[mem], g, base + 3, "mem", mem, n_mem)
        pending.append(finish(g, base + 3, "mem", mem, n_mem))
        e_full = jnp.concatenate([g[:, m, :] for m in range(MODES)], axis=1)
        z = spread(dot3(e_full, (qp[0], qp[1], qp[2])), 1 + step)
        pending.append(exchange_wait(tsend.at[step], t, base + 1))
        return [
            (t[i] - t[pos[i]]) - lanes_of(z, i) for i in range(SLOTS)
        ]

    def lane_sum(x):
        return jnp.sum(x, axis=1, keepdims=True)

    pending.append(finish(crall, 0, "mem", mem, n_mem))
    z = spread(dot3(pairs(crall), (qn[0], qn[1], qn[2])), 0)
    for i in range(SLOTS):
        lam[i] = lanes_of(z, i)
    kcopy.wait()
    zero = jnp.zeros((CASES, LANES), F32)
    terms = schur(lam)
    for i in range(SLOTS):
        s, j = divmod(i, 8)
        cut = slice(LANES * j, LANES * (j + 1))
        town[0, i] = rhs_ref[:, s, cut] - terms[s][:, cut]
    projected = reduce_start(0, (zero, zero))
    square = zero
    for i in range(SLOTS):
        p0[i] = projected[i]
        square = square + projected[i] * projected[i]

    terms = schur(p0)
    curve = zero
    for i in range(SLOTS):
        s, j = divmod(i, 8)
        value = terms[s][:, LANES * j : LANES * (j + 1)]
        town[1, i] = value
        curve = curve + value * p0[i]
    image = reduce_start(1, (curve, square))
    curvature = lane_sum(gb[1, :, MODES, :])
    norm = 0.5 * lane_sum(gb[1, :, MODES + 1, :])
    alpha = norm / curvature
    square = zero
    for i in range(SLOTS):
        value = p0[i] - alpha * image[i]
        p1[i] = value
        lam[i] = lam[i] + alpha * p0[i]
        square = square + value * value
    diagonal = lax.broadcasted_iota(jnp.int32, (CASES, LANES), 0) == lane
    as_row = jnp.sum(
        jnp.where(diagonal, lane_sum(square), 0.0), axis=0, keepdims=True
    )
    tm[mem] = as_row
    scatter(lambda peer: tm.at[mem], tm, 18, "mem", mem, n_mem)
    pending.append(finish(tm, 18, "mem", mem, n_mem))
    tr[rep] = total16(tm)
    scatter(lambda peer: tr.at[rep], tr, 19, "rep", rep, n_rep)
    pending.append(finish(tr, 19, "rep", rep, n_rep))
    fresh = 0.5 * lane_sum(
        jnp.where(diagonal, jnp.broadcast_to(total16(tr), (CASES, LANES)), 0.0)
    )
    beta = fresh / norm
    for i in range(SLOTS):
        d1[i] = p1[i] + beta * p0[i]

    terms = schur(d1)
    curve = zero
    for i in range(SLOTS):
        s, j = divmod(i, 8)
        value = terms[s][:, LANES * j : LANES * (j + 1)]
        town[2, i] = value
        curve = curve + value * d1[i]
    image = reduce_start(2, (curve, zero))
    alpha = fresh / lane_sum(gb[2, :, MODES, :])
    for i in range(SLOTS):
        s, j = divmod(i, 8)
        cut = slice(LANES * j, LANES * (j + 1))
        out_l[:, s, cut] = sgn[i] * (lam[i] + alpha * d1[i])
        out_p[:, s, cut] = sgn[i] * (p1[i] - alpha * image[i])

    for copy in pending:
        copy.wait_send()


def local(
    n_rep, n_mem,
    schur_blocks, rigid_modes, coarse_inverse, coarse_rhs, subdomain_rhs, partner, cluster_of,
):
    vmem = pl.BlockSpec(memory_space=pltpu.VMEM)
    smem = pl.BlockSpec(memory_space=pltpu.SMEM)
    out = jax.ShapeDtypeStruct((CASES, 2, 1024), F32)
    tile = (CASES, LANES)
    return pl.pallas_call(
        functools.partial(kernel, n_rep, n_mem),
        out_shape=(out, out),
        in_specs=[smem, smem, vmem, vmem, vmem, vmem, pl.BlockSpec(memory_space=pl.ANY)],
        out_specs=(vmem, vmem),
        scratch_shapes=[
            pltpu.VMEM((2, 1024, 1024), BF),
            pltpu.VMEM((3, ENT, 2048), BF),
            pltpu.VMEM((768, LANES), F32),
            pltpu.VMEM((3, 768, LANES), BF),
            pltpu.VMEM((3, 1024, LANES), BF),
            pltpu.VMEM((ENT, 768), BF),
            pltpu.VMEM((ENT, 1024), BF),
            pltpu.VMEM((2 * SLOTS, 8, LANES), F32),
            pltpu.VMEM((SLOTS, 8, LANES), F32),
            pltpu.VMEM((SLOTS, 8, LANES), F32),
            pltpu.VMEM((2 * SLOTS, *tile), F32),
            pltpu.VMEM((2 * SLOTS, *tile), F32),
            pltpu.VMEM((2 * SLOTS, *tile), F32),
            pltpu.VMEM((STEPS, SLOTS, *tile), F32),
            pltpu.VMEM((STEPS, SLOTS, *tile), F32),
            pltpu.VMEM(tile, F32),
            pltpu.VMEM((16, *tile), F32),
            pltpu.VMEM((1 + STEPS, 16, *tile), F32),
            pltpu.VMEM((STEPS, CASES, 8, LANES), F32),
            pltpu.VMEM((STEPS, 16, 8, LANES), F32),
            pltpu.VMEM((STEPS, 16, 8, LANES), F32),
            pltpu.VMEM((STEPS, 16, 8, LANES), F32),
            pltpu.VMEM((16, 1, LANES), F32),
            pltpu.VMEM((16, 1, LANES), F32),
            pltpu.VMEM((SLOTS, *tile), F32),
            pltpu.VMEM((SLOTS, *tile), F32),
            pltpu.VMEM((SLOTS, *tile), F32),
            pltpu.VMEM((SLOTS, *tile), F32),
            pltpu.SMEM((SLOTS,), jnp.int32),
            pltpu.SMEM((SLOTS,), jnp.int32),
            pltpu.SMEM((SLOTS,), jnp.int32),
            pltpu.SMEM((SLOTS,), jnp.int32),
            pltpu.SMEM((SLOTS,), F32),
            pltpu.SemaphoreType.DMA,
            pltpu.SemaphoreType.DMA((20,)),
            pltpu.SemaphoreType.DMA((20,)),
        ],
        compiler_params=pltpu.CompilerParams(
            collective_id=0, has_side_effects=True, vmem_limit_bytes=60 * 1024 * 1024
        ),
    )(
        partner, cluster_of, rigid_modes, coarse_inverse, coarse_rhs, subdomain_rhs,
        schur_blocks,
    )


def solution(mesh):
    placed = (
        P(("rep", "mem"), None, None),
        P(("rep", "mem"), None, None),
        P(None, "mem"),
        P(None, "mem"),
        P(None, ("rep", "mem"), None),
        P(("rep", "mem"), None),
        P(("rep", "mem")),
    )
    return jax.shard_map(
        functools.partial(local, mesh.shape["rep"], mesh.shape["mem"]),
        mesh=mesh,
        in_specs=placed,
        out_specs=(P(None, ("rep", "mem"), None), P(None, ("rep", "mem"), None)),
        check_vma=False,
    )
```

```python
import functools

import jax
import jax.numpy as jnp
from jax import lax
from jax.experimental import pallas as pl
from jax.experimental.pallas import tpu as pltpu
from jax.sharding import PartitionSpec as P

MESH = pl.DeviceIdType.MESH
F32 = jnp.float32
BF = jnp.bfloat16
CASES = 16
MODES = 6
SLOTS = 16
LANES = 128
STEPS = 3


def split3(x):
    hi = x.astype(BF)
    rest = x - hi.astype(F32)
    mid = rest.astype(BF)
    low = (rest - mid.astype(F32)).astype(BF)
    return hi, mid, low


def mm(a, b, nt=False):
    return lax.dot_general(
        a, b, (((1,), (1 if nt else 0,)), ((), ())), preferred_element_type=F32
    )


def dot3(x, w, nt=False):
    n = x.shape[0]
    a = jnp.concatenate(split3(x), axis=0)
    r1 = mm(a, w[0], nt)
    r2 = mm(a[: 2 * n], w[1], nt)
    r3 = mm(a[:n], w[2], nt)
    return r1[:n] + ((r1[n : 2 * n] + r2[:n]) + (r1[2 * n :] + r2[n:] + r3))


def dot_exact(x, onehot, nt=False):
    n = x.shape[0]
    r = mm(jnp.concatenate(split3(x), axis=0), onehot, nt)
    return r[:n] + (r[n : 2 * n] + r[2 * n :])


def total16(ref, *lead):
    parts = [ref[(*lead, i)] for i in range(16)]
    while len(parts) > 1:
        parts = [a + b for a, b in zip(parts[::2], parts[1::2])]
    return parts[0]


def kernel(
    n_rep, n_mem,
    partner_ref, cluster_ref, modes_ref, qinv_ref, crhs_ref, rhs_ref, schur_hbm,
    out_l, out_p,
    kbuf, wtf, wt, qf, qp, qs, ball, sc,
    gall, gown, gsend, tall0, tall1, tall2, town, tsend,
    crpad, crall, rowall, index_ref, yall, ysend, eb, rs, ra,
    tm, tr,
    lam, p0, p1, d1,
    key, code, pos, sslot, psub, sgn,
    ksem, send, recv,
):
    rep = lax.axis_index("rep")
    mem = lax.axis_index("mem")
    kcopy = pltpu.make_async_copy(schur_hbm, kbuf, ksem)
    kcopy.start()
    bar = pltpu.get_barrier_semaphore()

    def greet(axis, me, n):
        def body(off, _):
            pl.semaphore_signal(
                bar, inc=1, device_id={axis: me ^ off}, device_id_type=MESH
            )
            return 0
        lax.fori_loop(1, n, body, 0)

    greet("mem", mem, n_mem)
    greet("rep", rep, n_rep)

    def remote(src, dst, r, axis, peer):
        return pltpu.make_async_remote_copy(
            src_ref=src, dst_ref=dst, send_sem=send.at[r], recv_sem=recv.at[r],
            device_id={axis: peer}, device_id_type=MESH,
        )

    def scatter(src_of, dst, r, axis, me, n):
        def body(k, _):
            peer = me ^ (n - k)
            remote(src_of(peer), dst.at[me], r, axis, peer).start()
            return 0
        lax.fori_loop(1, n, body, 0)

    def finish(dst, r, axis, me, n):
        most = dst.at[pl.ds(0, n - 1)]
        copy = remote(most, most, r, axis, me ^ 1)
        copy.wait_recv()
        return copy

    def exchange_start(src, dst, r):
        for bit in (3, 2, 1, 0):
            remote(
                src.at[pl.ds(4 * bit, 4)], dst.at[pl.ds(SLOTS + 4 * bit, 4)],
                r, "mem", mem ^ (1 << bit),
            ).start()

    def exchange_wait(src, dst, r):
        copy = remote(src, dst.at[pl.ds(SLOTS, SLOTS)], r, "mem", mem ^ 1)
        copy.wait_recv()
        return copy

    for i in range(SLOTS):
        value = partner_ref[i // 8, i % 8]
        key[i] = value & (16 * n_mem - 1)
        psub[i] = ((value >> 3) & (2 * n_mem - 1)).astype(F32)
        first = (rep * n_mem + mem) * SLOTS + i < value
        sgn[i] = jnp.where(first, 1.0, -1.0).astype(F32)

    def table(i, _):
        mine = key[i]
        base = mine & ~15
        sent = jnp.int32(0)
        got = jnp.int32(0)
        for k in range(SLOTS):
            other = key[k]
            same = (other & ~15) == base
            sent += jnp.where(jnp.logical_and(same, other < mine), 1, 0)
            got += jnp.where(jnp.logical_and(same, i > k), 1, 0)
        diff = (mine >> 4) ^ mem
        bit = (
            jnp.where(diff >= 2, 4, 0) + jnp.where(diff >= 4, 4, 0)
            + jnp.where(diff >= 8, 4, 0)
        )
        here = diff == 0
        code[i] = jnp.where(here, -1, bit + sent)
        pos[i] = jnp.where(here, mine & 15, SLOTS + bit + (got & 3))
        return 0
    lax.fori_loop(0, SLOTS, table, 0)

    def places(p, _):
        found = jnp.int32(0)
        for k in range(SLOTS):
            found += jnp.where(code[k] == p, k, 0)
        sslot[p] = found & 15
        return 0
    lax.fori_loop(0, SLOTS, places, 0)

    for i in range(SLOTS):
        s, j = divmod(i, 8)
        value = modes_ref[:, s, LANES * j : LANES * (j + 1)]
        gown[i, 0:MODES, :] = value
        gall[i, 0:MODES, :] = value
    for p in range(SLOTS):
        gsend[p] = gown[sslot[p]]

    lane1 = lax.broadcasted_iota(jnp.int32, (1, LANES), 1)
    entry = (lane1 * 43) >> 8
    row = jnp.full((1, LANES), -1.0, F32)
    for i in range(SLOTS):
        row = jnp.where(entry == i, psub[i], row)
    for s in range(2):
        row = jnp.where(entry == SLOTS + s, (2 * mem + s).astype(F32), row)
        row = jnp.where(lane1 == 6 * 18 + s, cluster_ref[s].astype(F32), row)
    rowall[mem] = row

    odd = (mem & 1) == 1
    crpad[...] = jnp.zeros_like(crpad)
    crpad[:, 0:48] = crhs_ref[...]
    place = crpad[...]
    crall[mem] = jnp.where(odd, pltpu.roll(place, 64, 1), place)

    parts = split3(qinv_ref[...])
    for t in range(3):
        qs[48 * t : 48 * (t + 1), :] = parts[t]
    qf[...] = jnp.zeros_like(qf)
    half = pl.ds(pl.multiple_of(64 * (mem & 1), 64), 48)
    for m in range(16):
        qf[half, 64 * m : 64 * m + 48] = qinv_ref[:, 48 * m : 48 * (m + 1)]
    for j in range(8):
        cut = slice(LANES * j, LANES * (j + 1))
        parts = split3(qf[:, cut])
        for t in range(3):
            qp[t, :, cut] = parts[t]
    wtf[...] = jnp.zeros_like(wtf)
    ball[...] = jnp.zeros_like(ball)
    for i in range(SLOTS):
        s = i // 8
        wtf[96 + 6 * s : 102 + 6 * s, LANES * i : LANES * (i + 1)] = gown[i, 0:MODES, :]

    pl.semaphore_wait(bar, n_mem + n_rep - 2)

    pending = []
    scatter(lambda peer: crall.at[mem], crall, 0, "mem", mem, n_mem)
    scatter(lambda peer: rowall.at[mem], rowall, 20, "mem", mem, n_mem)
    exchange_start(gsend, gall, 1)

    def pairs(ref):
        return jnp.concatenate(
            [ref[2 * j] + ref[2 * j + 1] for j in range(8)], axis=1
        )

    def lanes_of(values, i):
        return values[:, LANES * i : LANES * (i + 1)]

    def schur(src):
        out = []
        for s in range(2):
            flat = jnp.concatenate(
                [src[8 * s + j].astype(BF) for j in range(8)], axis=1
            )
            out.append(mm(flat, kbuf[s]))
        return out

    def lane_sum(x):
        return jnp.sum(x, axis=1, keepdims=True)

    lane8 = lax.broadcasted_iota(jnp.int32, (8, LANES), 1)
    lane = lax.broadcasted_iota(jnp.int32, (CASES, LANES), 1)
    low = lane8 < 64

    def reduce_start(step, scalars):
        t = (tall0, tall1, tall2)[step]
        e = eb.at[step]
        base = 6 + 4 * step
        flat = jnp.concatenate([town[step, i] for i in range(SLOTS)], axis=1)
        own = dot3(flat, (wt[0], wt[1], wt[2]), nt=True)
        dense = dot_exact(own, sc[...])
        extra = jnp.zeros((8, LANES), F32)
        for k, value in enumerate(scalars):
            value = lane_sum(value)
            extra = jnp.where(lane8 == 48 + k, value[0:8], extra)
            extra = jnp.where(lane8 == 112 + k, value[8:16], extra)
        for j in range(8):
            tile = lanes_of(dense, j)
            up, down = tile[0:8], tile[8:16]
            e[2 * j] = jnp.where(low, up, pltpu.roll(down, 64, 1)) + extra
            e[2 * j + 1] = jnp.where(low, pltpu.roll(up, 64, 1), down) + extra
        rs[step, mem] = e[mem]
        scatter(lambda peer: e.at[peer], rs.at[step], base, "mem", mem, n_mem)
        for p in range(SLOTS):
            tsend[step, p] = town[step, sslot[p]]
        exchange_start(tsend.at[step], t, base + 1)
        for i in range(SLOTS):
            t[i] = town[step, i]
        pending.append(finish(rs.at[step], base, "mem", mem, n_mem))
        ra[step, rep] = total16(rs, step)
        scatter(lambda peer: ra.at[step, rep], ra.at[step], base + 2, "rep", rep, n_rep)
        pending.append(finish(ra.at[step], base + 2, "rep", rep, n_rep))
        tile = total16(ra, step)
        mine = jnp.concatenate([tile, pltpu.roll(tile, 64, 1)], axis=0)
        product = dot3(mine, (ball[0], ball[1], ball[2]))
        y = yall.at[1 + step]
        out = ysend.at[step]
        for m in range(16):
            out[m] = lanes_of(product, m)
        scatter(lambda peer: out.at[peer], y, base + 3, "mem", mem, n_mem)
        y[mem] = out[mem]
        pending.append(exchange_wait(tsend.at[step], t, base + 1))
        image = [t[i] - t[pos[i]] for i in range(SLOTS)]
        pending.append(finish(y, base + 3, "mem", mem, n_mem))
        z = dot3(total16(yall, 1 + step), (wt[0], wt[1], wt[2]))
        sums = [
            jnp.concatenate([mine[0:8, k : k + 1], mine[8:16, k : k + 1]], axis=0)
            for k in (48, 49)
        ]
        return [image[i] - lanes_of(z, i) for i in range(SLOTS)], sums

    pending.append(finish(crall, 0, "mem", mem, n_mem))
    y_slice = dot3(pairs(crall), (qp[0], qp[1], qp[2]), nt=True)
    yall[0, mem] = y_slice
    scatter(lambda peer: yall.at[0, mem], yall.at[0], 2, "mem", mem, n_mem)
    pending.append(finish(rowall, 20, "mem", mem, n_mem))
    cluster = jnp.full((16, LANES), -100.0, F32)
    rows = jnp.concatenate([rowall[m] for m in range(16)], axis=0)
    for m in range(16):
        for s in range(2):
            k = 6 * 18 + s
            number = jnp.broadcast_to(rows[m : m + 1, k : k + 1], (16, LANES))
            cluster = jnp.where(rows == 2.0 * m + s, number, cluster)
    entry16 = (lane * 43) >> 8
    mode16 = (lane - MODES * entry16).astype(F32)
    index = jnp.where(entry16 < 18, 6.0 * cluster + mode16, -100.0)
    for m in range(16):
        index_ref[m] = index[m : m + 1]
    column = jnp.transpose(jnp.broadcast_to(index_ref[mem], (LANES, LANES)))
    in_half = lax.broadcasted_iota(jnp.int32, (LANES, LANES), 1)
    whole = jnp.where(
        (in_half & 63) < 48, 48 * (in_half >> 6) + (in_half & 63), -1
    ).astype(F32)
    for j in range(8):
        hit = jnp.logical_and(whole >= 0.0, whole + 96.0 * j == column)
        sc[:, LANES * j : LANES * (j + 1)] = jnp.where(hit, 1.0, 0.0).astype(BF)

    pending.append(exchange_wait(gsend, gall, 1))
    for i in range(SLOTS):
        got = gall[pos[i]]
        wtf[6 * i : 6 * i + 6, LANES * i : LANES * (i + 1)] = -got[0:MODES]
    for i in range(SLOTS):
        cut = slice(LANES * i, LANES * (i + 1))
        parts = split3(wtf[:, cut])
        for t in range(3):
            wt[t, :, cut] = parts[t]

    number = lax.broadcasted_iota(jnp.int32, (768, LANES), 0).astype(F32)
    for m in range(16):
        hit = number == jnp.broadcast_to(index_ref[m], (768, LANES))
        chosen = mm(qs[...], jnp.where(hit, 1.0, 0.0).astype(BF))
        for t in range(3):
            ball[t, 0:48, LANES * m : LANES * (m + 1)] = (
                chosen[48 * t : 48 * (t + 1)].astype(BF)
            )

    pending.append(finish(yall.at[0], 2, "mem", mem, n_mem))
    picked = dot_exact(pairs(yall.at[0]), sc[...], nt=True)
    z = dot3(picked, (wt[0], wt[1], wt[2]))
    for i in range(SLOTS):
        lam[i] = lanes_of(z, i)
    kcopy.wait()
    zero = jnp.zeros((CASES, LANES), F32)
    terms = schur(lam)
    for i in range(SLOTS):
        s, j = divmod(i, 8)
        cut = slice(LANES * j, LANES * (j + 1))
        town[0, i] = rhs_ref[:, s, cut] - terms[s][:, cut]
    projected, _ = reduce_start(0, ())
    square = zero
    for i in range(SLOTS):
        p0[i] = projected[i]
        square = square + projected[i] * projected[i]

    terms = schur(p0)
    curve = zero
    for i in range(SLOTS):
        s, j = divmod(i, 8)
        value = terms[s][:, LANES * j : LANES * (j + 1)]
        town[1, i] = value
        curve = curve + value * p0[i]
    image, (curvature, norm) = reduce_start(1, (curve, square))
    norm = 0.5 * norm
    alpha = norm / curvature
    square = zero
    for i in range(SLOTS):
        value = p0[i] - alpha * image[i]
        p1[i] = value
        square = square + value * value
    diagonal = lax.broadcasted_iota(jnp.int32, (CASES, LANES), 0) == lane
    as_row = jnp.sum(
        jnp.where(diagonal, lane_sum(square), 0.0), axis=0, keepdims=True
    )
    tm[mem] = as_row
    scatter(lambda peer: tm.at[mem], tm, 18, "mem", mem, n_mem)
    for i in range(SLOTS):
        lam[i] = lam[i] + alpha * p0[i]
    pending.append(finish(tm, 18, "mem", mem, n_mem))
    tr[rep] = total16(tm)
    scatter(lambda peer: tr.at[rep], tr, 19, "rep", rep, n_rep)
    pending.append(finish(tr, 19, "rep", rep, n_rep))
    fresh = 0.5 * lane_sum(
        jnp.where(diagonal, jnp.broadcast_to(total16(tr), (CASES, LANES)), 0.0)
    )
    beta = fresh / norm
    for i in range(SLOTS):
        d1[i] = p1[i] + beta * p0[i]

    terms = schur(d1)
    curve = zero
    for i in range(SLOTS):
        s, j = divmod(i, 8)
        value = terms[s][:, LANES * j : LANES * (j + 1)]
        town[2, i] = value
        curve = curve + value * d1[i]
    image, (curvature, _) = reduce_start(2, (curve,))
    alpha = fresh / curvature
    for i in range(SLOTS):
        s, j = divmod(i, 8)
        cut = slice(LANES * j, LANES * (j + 1))
        out_l[:, s, cut] = sgn[i] * (lam[i] + alpha * d1[i])
        out_p[:, s, cut] = sgn[i] * (p1[i] - alpha * image[i])

    for copy in pending:
        copy.wait_send()


def local(
    n_rep, n_mem,
    schur_blocks, rigid_modes, coarse_inverse, coarse_rhs, subdomain_rhs, partner, cluster_of,
):
    vmem = pl.BlockSpec(memory_space=pltpu.VMEM)
    smem = pl.BlockSpec(memory_space=pltpu.SMEM)
    out = jax.ShapeDtypeStruct((CASES, 2, 1024), F32)
    tile = (CASES, LANES)
    return pl.pallas_call(
        functools.partial(kernel, n_rep, n_mem),
        out_shape=(out, out),
        in_specs=[smem, smem, vmem, vmem, vmem, vmem, pl.BlockSpec(memory_space=pl.ANY)],
        out_specs=(vmem, vmem),
        scratch_shapes=[
            pltpu.VMEM((2, 1024, 1024), BF),
            pltpu.VMEM((LANES, 2048), F32),
            pltpu.VMEM((3, LANES, 2048), BF),
            pltpu.VMEM((LANES, 1024), F32),
            pltpu.VMEM((3, LANES, 1024), BF),
            pltpu.VMEM((144, 768), BF),
            pltpu.VMEM((3, LANES, 2048), BF),
            pltpu.VMEM((LANES, 1024), BF),
            pltpu.VMEM((2 * SLOTS, 8, LANES), F32),
            pltpu.VMEM((SLOTS, 8, LANES), F32),
            pltpu.VMEM((SLOTS, 8, LANES), F32),
            pltpu.VMEM((2 * SLOTS, *tile), F32),
            pltpu.VMEM((2 * SLOTS, *tile), F32),
            pltpu.VMEM((2 * SLOTS, *tile), F32),
            pltpu.VMEM((STEPS, SLOTS, *tile), F32),
            pltpu.VMEM((STEPS, SLOTS, *tile), F32),
            pltpu.VMEM(tile, F32),
            pltpu.VMEM((16, *tile), F32),
            pltpu.VMEM((16, 1, LANES), F32),
            pltpu.VMEM((16, 1, LANES), F32),
            pltpu.VMEM((1 + STEPS, 16, *tile), F32),
            pltpu.VMEM((STEPS, 16, *tile), F32),
            pltpu.VMEM((STEPS, 16, 8, LANES), F32),
            pltpu.VMEM((STEPS, 16, 8, LANES), F32),
            pltpu.VMEM((STEPS, 16, 8, LANES), F32),
            pltpu.VMEM((16, 1, LANES), F32),
            pltpu.VMEM((16, 1, LANES), F32),
            pltpu.VMEM((SLOTS, *tile), F32),
            pltpu.VMEM((SLOTS, *tile), F32),
            pltpu.VMEM((SLOTS, *tile), F32),
            pltpu.VMEM((SLOTS, *tile), F32),
            pltpu.SMEM((SLOTS,), jnp.int32),
            pltpu.SMEM((SLOTS,), jnp.int32),
            pltpu.SMEM((SLOTS,), jnp.int32),
            pltpu.SMEM((SLOTS,), jnp.int32),
            pltpu.SMEM((SLOTS,), F32),
            pltpu.SMEM((SLOTS,), F32),
            pltpu.SemaphoreType.DMA,
            pltpu.SemaphoreType.DMA((21,)),
            pltpu.SemaphoreType.DMA((21,)),
        ],
        compiler_params=pltpu.CompilerParams(
            collective_id=0, has_side_effects=True, vmem_limit_bytes=60 * 1024 * 1024
        ),
    )(
        partner, cluster_of, jnp.swapaxes(rigid_modes, 0, 1), coarse_inverse.T, coarse_rhs, subdomain_rhs,
        schur_blocks,
    )


def solution(mesh):
    placed = (
        P(("rep", "mem"), None, None),
        P(("rep", "mem"), None, None),
        P(None, "mem"),
        P(None, "mem"),
        P(None, ("rep", "mem"), None),
        P(("rep", "mem"), None),
        P(("rep", "mem")),
    )
    return jax.shard_map(
        functools.partial(local, mesh.shape["rep"], mesh.shape["mem"]),
        mesh=mesh,
        in_specs=placed,
        out_specs=(P(None, ("rep", "mem"), None), P(None, ("rep", "mem"), None)),
        check_vma=False,
    )
```

```python
import functools

import jax
import jax.numpy as jnp
from jax import lax
from jax.experimental import pallas as pl
from jax.experimental.pallas import tpu as pltpu
from jax.sharding import PartitionSpec as P

MESH = pl.DeviceIdType.MESH
F32 = jnp.float32
BF = jnp.bfloat16
CASES = 16
MODES = 6
SLOTS = 16
LANES = 128
STEPS = 3


def split3(x):
    hi = x.astype(BF)
    rest = x - hi.astype(F32)
    mid = rest.astype(BF)
    low = (rest - mid.astype(F32)).astype(BF)
    return hi, mid, low


def mm(a, b, nt=False):
    return lax.dot_general(
        a, b, (((1,), (1 if nt else 0,)), ((), ())), preferred_element_type=F32
    )


def dot3(x, w, nt=False):
    n = x.shape[0]
    a = jnp.concatenate(split3(x), axis=0)
    r1 = mm(a, w[0], nt)
    r2 = mm(a[: 2 * n], w[1], nt)
    r3 = mm(a[:n], w[2], nt)
    return r1[:n] + ((r1[n : 2 * n] + r2[:n]) + (r1[2 * n :] + r2[n:] + r3))


def dot_exact(x, onehot, nt=False):
    n = x.shape[0]
    r = mm(jnp.concatenate(split3(x), axis=0), onehot, nt)
    return r[:n] + (r[n : 2 * n] + r[2 * n :])


def total16(ref, *lead):
    parts = [ref[(*lead, i)] for i in range(16)]
    while len(parts) > 1:
        parts = [a + b for a, b in zip(parts[::2], parts[1::2])]
    return parts[0]


def kernel(
    n_rep, n_mem,
    partner_ref, cluster_ref, modes_hbm, qinv_hbm, crhs_hbm, rhs_hbm, schur_hbm,
    outs,
    modes_ref, qinv_ref, crhs_ref, rhs_ref,
    kbuf, wtf, wt, qf, qp, qs, ball, sc,
    gall, gown, gsend, tall0, tall1, tall2, town, tsend,
    crpad, crall, start, index_ref, yall, ysend, eb, rs, ra,
    tm, tr,
    lam, p0, p1, d1,
    key, code, pos, sslot, psub, sgn,
    ksem, send, recv,
):
    rep = lax.axis_index("rep")
    mem = lax.axis_index("mem")
    bar = pltpu.get_barrier_semaphore()

    def greet(axis, me, n):
        def body(off, _):
            pl.semaphore_signal(
                bar, inc=1, device_id={axis: me ^ off}, device_id_type=MESH
            )
            return 0
        lax.fori_loop(1, n, body, 0)

    greet("mem", mem, n_mem)
    greet("rep", rep, n_rep)
    inputs = [
        pltpu.make_async_copy(modes_hbm, modes_ref, ksem.at[0]),
        pltpu.make_async_copy(crhs_hbm, crhs_ref, ksem.at[1]),
        pltpu.make_async_copy(qinv_hbm, qinv_ref, ksem.at[2]),
        pltpu.make_async_copy(rhs_hbm, rhs_ref, ksem.at[3]),
    ]
    for copy in inputs:
        copy.start()
    kcopy = pltpu.make_async_copy(schur_hbm, kbuf, ksem.at[4])
    kcopy.start()

    def remote(src, dst, r, axis, peer):
        return pltpu.make_async_remote_copy(
            src_ref=src, dst_ref=dst, send_sem=send.at[r], recv_sem=recv.at[r],
            device_id={axis: peer}, device_id_type=MESH,
        )

    def scatter(src_of, dst, r, axis, me, n):
        def body(k, _):
            peer = me ^ (n - k)
            remote(src_of(peer), dst.at[me], r, axis, peer).start()
            return 0
        lax.fori_loop(1, n, body, 0)

    def finish(dst, r, axis, me, n):
        most = dst.at[pl.ds(0, n - 1)]
        copy = remote(most, most, r, axis, me ^ 1)
        copy.wait_recv()
        return copy

    def exchange_start(src, dst, r):
        for bit in (3, 2, 1, 0):
            remote(
                src.at[pl.ds(4 * bit, 4)], dst.at[pl.ds(SLOTS + 4 * bit, 4)],
                r, "mem", mem ^ (1 << bit),
            ).start()

    def exchange_wait(src, dst, r):
        copy = remote(src, dst.at[pl.ds(SLOTS, SLOTS)], r, "mem", mem ^ 1)
        copy.wait_recv()
        return copy

    for i in range(SLOTS):
        value = partner_ref[i // 8, i % 8]
        key[i] = value & (16 * n_mem - 1)
        psub[i] = ((value >> 3) & (2 * n_mem - 1)).astype(F32)
        first = (rep * n_mem + mem) * SLOTS + i < value
        sgn[i] = jnp.where(first, 1.0, -1.0).astype(F32)

    def table(i, _):
        mine = key[i]
        base = mine & ~15
        sent = jnp.int32(0)
        got = jnp.int32(0)
        for k in range(SLOTS):
            other = key[k]
            same = (other & ~15) == base
            sent += jnp.where(jnp.logical_and(same, other < mine), 1, 0)
            got += jnp.where(jnp.logical_and(same, i > k), 1, 0)
        diff = (mine >> 4) ^ mem
        bit = (
            jnp.where(diff >= 2, 4, 0) + jnp.where(diff >= 4, 4, 0)
            + jnp.where(diff >= 8, 4, 0)
        )
        here = diff == 0
        code[i] = jnp.where(here, -1, bit + sent)
        pos[i] = jnp.where(here, mine & 15, SLOTS + bit + (got & 3))
        return 0
    lax.fori_loop(0, SLOTS, table, 0)

    def places(p, _):
        found = jnp.int32(0)
        for k in range(SLOTS):
            found += jnp.where(code[k] == p, k, 0)
        sslot[p] = found & 15
        return 0
    lax.fori_loop(0, SLOTS, places, 0)

    inputs[0].wait()
    for i in range(SLOTS):
        s, j = divmod(i, 8)
        value = modes_ref[:, s, LANES * j : LANES * (j + 1)]
        gown[i, 0:MODES, :] = value
        gall[i, 0:MODES, :] = value
    for p in range(SLOTS):
        gsend[p] = gown[sslot[p]]

    lane8 = lax.broadcasted_iota(jnp.int32, (8, LANES), 1)
    lane = lax.broadcasted_iota(jnp.int32, (CASES, LANES), 1)
    low = lane8 < 64

    def pack(x):
        return jnp.where(low, x[0:8], pltpu.roll(x[8:16], 64, 1))

    def unpack(ref):
        out = []
        for j in range(8):
            left, right = ref[2 * j], ref[2 * j + 1]
            up = jnp.where(low, left, pltpu.roll(right, 64, 1))
            down = jnp.where(low, pltpu.roll(left, 64, 1), right)
            out.append(jnp.concatenate([up, down], axis=0))
        return jnp.concatenate(out, axis=1)

    crpad[...] = jnp.zeros_like(crpad)
    inputs[1].wait()
    crpad[:, 0:48] = crhs_ref[...]
    place = pack(crpad[...])
    for i in range(SLOTS):
        place = jnp.where(lane8 == 48 + i, psub[i], place)
    for s in range(2):
        place = jnp.where(lane8 == 112 + s, cluster_ref[s].astype(F32), place)
    crall[mem] = place

    inputs[2].wait()
    parts = split3(qinv_ref[...])
    for t in range(3):
        qs[48 * t : 48 * (t + 1), :] = parts[t]
    qf[...] = jnp.zeros_like(qf)
    for m in range(16):
        qf[0:48, 64 * m : 64 * m + 48] = qinv_ref[:, 48 * m : 48 * (m + 1)]
    for j in range(8):
        cut = slice(LANES * j, LANES * (j + 1))
        parts = split3(qf[:, cut])
        for t in range(3):
            qp[t, :, cut] = parts[t]
    wtf[...] = jnp.zeros_like(wtf)
    ball[...] = jnp.zeros_like(ball)
    for i in range(SLOTS):
        s = i // 8
        wtf[96 + 6 * s : 102 + 6 * s, LANES * i : LANES * (i + 1)] = gown[i, 0:MODES, :]

    pl.semaphore_wait(bar, n_mem + n_rep - 2)

    pending = []
    scatter(lambda peer: crall.at[mem], crall, 0, "mem", mem, n_mem)
    exchange_start(gsend, gall, 1)

    def lanes_of(values, i):
        return values[:, LANES * i : LANES * (i + 1)]

    def schur(src):
        out = []
        for s in range(2):
            flat = jnp.concatenate(
                [src[8 * s + j].astype(BF) for j in range(8)], axis=1
            )
            out.append(mm(flat, kbuf[s]))
        return out

    def lane_sum(x):
        return jnp.sum(x, axis=1, keepdims=True)

    def reduce_start(step, scalars):
        t = (tall0, tall1, tall2)[step]
        e = eb.at[step]
        base = 6 + 4 * step
        flat = jnp.concatenate([town[step, i] for i in range(SLOTS)], axis=1)
        own = dot3(flat, (wt[0], wt[1], wt[2]), nt=True)
        dense = dot_exact(own, sc[...])
        extra = jnp.zeros((8, LANES), F32)
        for k, value in enumerate(scalars):
            value = lane_sum(value)
            extra = jnp.where(lane8 == 48 + k, value[0:8], extra)
            extra = jnp.where(lane8 == 112 + k, value[8:16], extra)
        for j in range(8):
            tile = lanes_of(dense, j)
            up, down = tile[0:8], tile[8:16]
            e[2 * j] = pack(tile) + extra
            e[2 * j + 1] = jnp.where(low, pltpu.roll(up, 64, 1), down) + extra
        rs[step, mem] = e[mem]
        scatter(lambda peer: e.at[peer], rs.at[step], base, "mem", mem, n_mem)
        for p in range(SLOTS):
            tsend[step, p] = town[step, sslot[p]]
        for i in range(SLOTS):
            t[i] = town[step, i]
        pending.append(finish(rs.at[step], base, "mem", mem, n_mem))
        ra[step, rep] = total16(rs, step)
        scatter(lambda peer: ra.at[step, rep], ra.at[step], base + 2, "rep", rep, n_rep)
        exchange_start(tsend.at[step], t, base + 1)
        pending.append(finish(ra.at[step], base + 2, "rep", rep, n_rep))
        tile = total16(ra, step)
        mine = jnp.concatenate([tile, pltpu.roll(tile, 64, 1)], axis=0)
        product = dot3(mine, (ball[0], ball[1], ball[2]))
        y = yall.at[step]
        out = ysend.at[step]
        for m in range(16):
            out[m] = lanes_of(product, m)
        scatter(lambda peer: out.at[peer], y, base + 3, "mem", mem, n_mem)
        y[mem] = out[mem]
        pending.append(exchange_wait(tsend.at[step], t, base + 1))
        image = [t[i] - t[pos[i]] for i in range(SLOTS)]
        pending.append(finish(y, base + 3, "mem", mem, n_mem))
        z = dot3(total16(yall, step), (wt[0], wt[1], wt[2]))
        sums = [
            jnp.concatenate([mine[0:8, k : k + 1], mine[8:16, k : k + 1]], axis=0)
            for k in (48, 49)
        ]
        return [image[i] - lanes_of(z, i) for i in range(SLOTS)], sums

    pending.append(finish(crall, 0, "mem", mem, n_mem))
    y_slice = dot3(unpack(crall), (qp[0], qp[1], qp[2]), nt=True)
    start[mem] = pack(y_slice)
    scatter(lambda peer: start.at[mem], start, 2, "mem", mem, n_mem)
    heads = jnp.concatenate([crall[m][0:1] for m in range(16)], axis=0)
    source = lax.broadcasted_iota(jnp.int32, (LANES, LANES), 0)
    wanted = 48 + ((lax.broadcasted_iota(jnp.int32, (LANES, LANES), 1) * 43) >> 8)
    widen = jnp.where(source == wanted, 1.0, 0.0).astype(BF)
    rows = mm(heads.astype(BF), widen)
    member = 2 * lax.broadcasted_iota(jnp.int32, (16, LANES), 0).astype(F32)
    for s in range(2):
        own_lane = ((lane * 43) >> 8) == SLOTS + s
        rows = jnp.where(own_lane, member + float(s), rows)
    cluster = jnp.full((16, LANES), -100.0, F32)
    for m in range(16):
        for s in range(2):
            k = 112 + s
            number = jnp.broadcast_to(heads[m : m + 1, k : k + 1], (16, LANES))
            cluster = jnp.where(rows == 2.0 * m + s, number, cluster)
    entry16 = (lane * 43) >> 8
    mode16 = (lane - MODES * entry16).astype(F32)
    index = jnp.where(entry16 < 18, 6.0 * cluster + mode16, -100.0)
    for m in range(16):
        index_ref[m] = index[m : m + 1]
    column = jnp.transpose(jnp.broadcast_to(index_ref[mem], (LANES, LANES)))
    in_half = lax.broadcasted_iota(jnp.int32, (LANES, LANES), 1)
    whole = jnp.where(
        (in_half & 63) < 48, 48 * (in_half >> 6) + (in_half & 63), -1
    ).astype(F32)
    for j in range(8):
        hit = jnp.logical_and(whole >= 0.0, whole + 96.0 * j == column)
        sc[:, LANES * j : LANES * (j + 1)] = jnp.where(hit, 1.0, 0.0).astype(BF)

    pending.append(exchange_wait(gsend, gall, 1))
    for i in range(SLOTS):
        got = gall[pos[i]]
        wtf[6 * i : 6 * i + 6, LANES * i : LANES * (i + 1)] = -got[0:MODES]
    for i in range(SLOTS):
        cut = slice(LANES * i, LANES * (i + 1))
        parts = split3(wtf[:, cut])
        for t in range(3):
            wt[t, :, cut] = parts[t]

    number = lax.broadcasted_iota(jnp.int32, (768, LANES), 0).astype(F32)
    for m in range(16):
        hit = number == jnp.broadcast_to(index_ref[m], (768, LANES))
        chosen = mm(qs[...], jnp.where(hit, 1.0, 0.0).astype(BF))
        for t in range(3):
            ball[t, 0:48, LANES * m : LANES * (m + 1)] = (
                chosen[48 * t : 48 * (t + 1)].astype(BF)
            )

    pending.append(finish(start, 2, "mem", mem, n_mem))
    picked = dot_exact(unpack(start), sc[...], nt=True)
    z = dot3(picked, (wt[0], wt[1], wt[2]))
    for i in range(SLOTS):
        lam[i] = lanes_of(z, i)
    inputs[3].wait()
    kcopy.wait()
    zero = jnp.zeros((CASES, LANES), F32)
    terms = schur(lam)
    for i in range(SLOTS):
        s, j = divmod(i, 8)
        cut = slice(LANES * j, LANES * (j + 1))
        town[0, i] = rhs_ref[:, s, cut] - terms[s][:, cut]
    projected, _ = reduce_start(0, ())
    square = zero
    for i in range(SLOTS):
        p0[i] = projected[i]
        square = square + projected[i] * projected[i]

    terms = schur(p0)
    curve = zero
    for i in range(SLOTS):
        s, j = divmod(i, 8)
        value = terms[s][:, LANES * j : LANES * (j + 1)]
        town[1, i] = value
        curve = curve + value * p0[i]
    image, (curvature, norm) = reduce_start(1, (curve, square))
    norm = 0.5 * norm
    alpha = norm / curvature
    square = zero
    for i in range(SLOTS):
        value = p0[i] - alpha * image[i]
        p1[i] = value
        square = square + value * value
    diagonal = lax.broadcasted_iota(jnp.int32, (CASES, LANES), 0) == lane
    as_row = jnp.sum(
        jnp.where(diagonal, lane_sum(square), 0.0), axis=0, keepdims=True
    )
    tm[mem] = as_row
    scatter(lambda peer: tm.at[mem], tm, 18, "mem", mem, n_mem)
    for i in range(SLOTS):
        lam[i] = lam[i] + alpha * p0[i]
    pending.append(finish(tm, 18, "mem", mem, n_mem))
    tr[rep] = total16(tm)
    scatter(lambda peer: tr.at[rep], tr, 19, "rep", rep, n_rep)
    pending.append(finish(tr, 19, "rep", rep, n_rep))
    fresh = 0.5 * lane_sum(
        jnp.where(diagonal, jnp.broadcast_to(total16(tr), (CASES, LANES)), 0.0)
    )
    beta = fresh / norm
    for i in range(SLOTS):
        d1[i] = p1[i] + beta * p0[i]

    terms = schur(d1)
    curve = zero
    for i in range(SLOTS):
        s, j = divmod(i, 8)
        value = terms[s][:, LANES * j : LANES * (j + 1)]
        town[2, i] = value
        curve = curve + value * d1[i]
    image, (curvature, _) = reduce_start(2, (curve,))
    alpha = fresh / curvature
    for i in range(SLOTS):
        s, j = divmod(i, 8)
        cut = slice(LANES * j, LANES * (j + 1))
        outs[0, :, s, cut] = sgn[i] * (lam[i] + alpha * d1[i])
        outs[1, :, s, cut] = sgn[i] * (p1[i] - alpha * image[i])

    for copy in pending:
        copy.wait_send()


def local(
    n_rep, n_mem,
    schur_blocks, rigid_modes, coarse_inverse, coarse_rhs, subdomain_rhs, partner, cluster_of,
):
    vmem = pl.BlockSpec(memory_space=pltpu.VMEM)
    smem = pl.BlockSpec(memory_space=pltpu.SMEM)
    out = jax.ShapeDtypeStruct((2, CASES, 2, 1024), F32)
    tile = (CASES, LANES)
    found = pl.pallas_call(
        functools.partial(kernel, n_rep, n_mem),
        out_shape=out,
        in_specs=[smem, smem] + [pl.BlockSpec(memory_space=pl.ANY)] * 5,
        out_specs=vmem,
        scratch_shapes=[
            pltpu.VMEM((MODES, 2, 1024), F32),
            pltpu.VMEM((48, 768), F32),
            pltpu.VMEM((CASES, 48), F32),
            pltpu.VMEM((CASES, 2, 1024), F32),
            pltpu.VMEM((2, 1024, 1024), BF),
            pltpu.VMEM((LANES, 2048), F32),
            pltpu.VMEM((3, LANES, 2048), BF),
            pltpu.VMEM((LANES, 1024), F32),
            pltpu.VMEM((3, LANES, 1024), BF),
            pltpu.VMEM((144, 768), BF),
            pltpu.VMEM((3, LANES, 2048), BF),
            pltpu.VMEM((LANES, 1024), BF),
            pltpu.VMEM((2 * SLOTS, MODES, LANES), F32),
            pltpu.VMEM((SLOTS, MODES, LANES), F32),
            pltpu.VMEM((SLOTS, MODES, LANES), F32),
            pltpu.VMEM((2 * SLOTS, *tile), F32),
            pltpu.VMEM((2 * SLOTS, *tile), F32),
            pltpu.VMEM((2 * SLOTS, *tile), F32),
            pltpu.VMEM((STEPS, SLOTS, *tile), F32),
            pltpu.VMEM((STEPS, SLOTS, *tile), F32),
            pltpu.VMEM(tile, F32),
            pltpu.VMEM((16, 8, LANES), F32),
            pltpu.VMEM((16, 8, LANES), F32),
            pltpu.VMEM((16, 1, LANES), F32),
            pltpu.VMEM((STEPS, 16, *tile), F32),
            pltpu.VMEM((STEPS, 16, *tile), F32),
            pltpu.VMEM((STEPS, 16, 8, LANES), F32),
            pltpu.VMEM((STEPS, 16, 8, LANES), F32),
            pltpu.VMEM((STEPS, 16, 8, LANES), F32),
            pltpu.VMEM((16, 1, LANES), F32),
            pltpu.VMEM((16, 1, LANES), F32),
            pltpu.VMEM((SLOTS, *tile), F32),
            pltpu.VMEM((SLOTS, *tile), F32),
            pltpu.VMEM((SLOTS, *tile), F32),
            pltpu.VMEM((SLOTS, *tile), F32),
            pltpu.SMEM((SLOTS,), jnp.int32),
            pltpu.SMEM((SLOTS,), jnp.int32),
            pltpu.SMEM((SLOTS,), jnp.int32),
            pltpu.SMEM((SLOTS,), jnp.int32),
            pltpu.SMEM((SLOTS,), F32),
            pltpu.SMEM((SLOTS,), F32),
            pltpu.SemaphoreType.DMA((5,)),
            pltpu.SemaphoreType.DMA((20,)),
            pltpu.SemaphoreType.DMA((20,)),
        ],
        compiler_params=pltpu.CompilerParams(
            collective_id=0, has_side_effects=True, vmem_limit_bytes=60 * 1024 * 1024
        ),
    )(
        partner, cluster_of, jnp.swapaxes(rigid_modes, 0, 1), coarse_inverse.T, coarse_rhs, subdomain_rhs,
        schur_blocks,
    )
    return found[0], found[1]


def solution(mesh):
    placed = (
        P(("rep", "mem"), None, None),
        P(("rep", "mem"), None, None),
        P(None, "mem"),
        P(None, "mem"),
        P(None, ("rep", "mem"), None),
        P(("rep", "mem"), None),
        P(("rep", "mem")),
    )
    return jax.shard_map(
        functools.partial(local, mesh.shape["rep"], mesh.shape["mem"]),
        mesh=mesh,
        in_specs=placed,
        out_specs=(P(None, ("rep", "mem"), None), P(None, ("rep", "mem"), None)),
        check_vma=False,
    )
```

```python
import functools

import jax
import jax.numpy as jnp
from jax import lax
from jax.experimental import pallas as pl
from jax.experimental.pallas import tpu as pltpu
from jax.sharding import PartitionSpec as P

MESH = pl.DeviceIdType.MESH
F32 = jnp.float32
BF = jnp.bfloat16
CASES = 16
MODES = 6
SLOTS = 16
LANES = 128
STEPS = 3


def split3(x):
    hi = x.astype(BF)
    rest = x - hi.astype(F32)
    mid = rest.astype(BF)
    low = (rest - mid.astype(F32)).astype(BF)
    return hi, mid, low


def mm(a, b, nt=False):
    return lax.dot_general(
        a, b, (((1,), (1 if nt else 0,)), ((), ())), preferred_element_type=F32
    )


def dot3(x, w, nt=False):
    n = x.shape[0]
    a = jnp.concatenate(split3(x), axis=0)
    r1 = mm(a, w[0], nt)
    r2 = mm(a[: 2 * n], w[1], nt)
    r3 = mm(a[:n], w[2], nt)
    return r1[:n] + ((r1[n : 2 * n] + r2[:n]) + (r1[2 * n :] + r2[n:] + r3))


def dot_exact(x, onehot, nt=False):
    n = x.shape[0]
    r = mm(jnp.concatenate(split3(x), axis=0), onehot, nt)
    return r[:n] + (r[n : 2 * n] + r[2 * n :])


def total16(ref, *lead):
    parts = [ref[(*lead, i)] for i in range(16)]
    while len(parts) > 1:
        parts = [a + b for a, b in zip(parts[::2], parts[1::2])]
    return parts[0]


def kernel(
    n_rep, n_mem,
    partner_ref, cluster_ref, modes_hbm, qinv_hbm, crhs_hbm, rhs_hbm, schur_hbm,
    outs,
    modes_ref, qinv_ref, crhs_ref, rhs_ref,
    kbuf, wtf, wt, qf, qp, qs, ball, sc,
    gall, gown, gsend, tall0, tall1, tall2, town, tsend,
    crpad, crall, start, index_ref, yall, ysend, eb, rs, ra,
    tm, tr,
    lam, p0, p1, d1,
    key, code, pos, sslot, psub, sgn,
    ksem, send, recv,
):
    rep = lax.axis_index("rep")
    mem = lax.axis_index("mem")
    far = 1 - (mem >> 3)
    bar = pltpu.get_barrier_semaphore()

    def greet(axis, me, n):
        def body(off, _):
            pl.semaphore_signal(
                bar, inc=1, device_id={axis: me ^ off}, device_id_type=MESH
            )
            return 0
        lax.fori_loop(1, n, body, 0)

    greet("mem", mem, n_mem)
    greet("rep", rep, n_rep)
    inputs = [
        pltpu.make_async_copy(modes_hbm, modes_ref, ksem.at[0]),
        pltpu.make_async_copy(crhs_hbm, crhs_ref, ksem.at[1]),
        pltpu.make_async_copy(qinv_hbm, qinv_ref, ksem.at[2]),
        pltpu.make_async_copy(rhs_hbm, rhs_ref, ksem.at[3]),
    ]
    for copy in inputs:
        copy.start()
    kcopy = pltpu.make_async_copy(schur_hbm, kbuf, ksem.at[4])
    kcopy.start()

    def remote(src, dst, r, axis, peer):
        return pltpu.make_async_remote_copy(
            src_ref=src, dst_ref=dst, send_sem=send.at[r], recv_sem=recv.at[r],
            device_id={axis: peer}, device_id_type=MESH,
        )

    def scatter(src_of, dst, r, axis, me, n, first=1, last=16):
        def body(k, _):
            peer = me ^ (n - k)
            remote(src_of(peer), dst.at[me], r, axis, peer).start()
            return 0
        lax.fori_loop(first, min(n, last), body, 0, unroll=3)

    def finish(dst, r, axis, me, n):
        most = dst.at[pl.ds(0, n - 1)]
        copy = remote(most, most, r, axis, me ^ 1)
        copy.wait_recv()
        return copy

    def exchange_start(src, dst, r):
        for bit in (3, 2, 1, 0):
            remote(
                src.at[pl.ds(4 * bit, 4)], dst.at[pl.ds(SLOTS + 4 * bit, 4)],
                r, "mem", mem ^ (1 << bit),
            ).start()

    def exchange_wait(src, dst, r):
        copy = remote(src, dst.at[pl.ds(SLOTS, SLOTS)], r, "mem", mem ^ 1)
        copy.wait_recv()
        return copy

    for i in range(SLOTS):
        value = partner_ref[i // 8, i % 8]
        key[i] = value & (16 * n_mem - 1)
        psub[i] = ((value >> 3) & (2 * n_mem - 1)).astype(F32)
        first = (rep * n_mem + mem) * SLOTS + i < value
        sgn[i] = jnp.where(first, 1.0, -1.0).astype(F32)

    def table(i, _):
        mine = key[i]
        base = mine & ~15
        sent = jnp.int32(0)
        got = jnp.int32(0)
        for k in range(SLOTS):
            other = key[k]
            same = (other & ~15) == base
            sent += jnp.where(jnp.logical_and(same, other < mine), 1, 0)
            got += jnp.where(jnp.logical_and(same, i > k), 1, 0)
        diff = (mine >> 4) ^ mem
        bit = (
            jnp.where(diff >= 2, 4, 0) + jnp.where(diff >= 4, 4, 0)
            + jnp.where(diff >= 8, 4, 0)
        )
        here = diff == 0
        code[i] = jnp.where(here, -1, bit + sent)
        pos[i] = jnp.where(here, mine & 15, SLOTS + bit + (got & 3))
        return 0
    lax.fori_loop(0, SLOTS, table, 0)

    def places(p, _):
        found = jnp.int32(0)
        for k in range(SLOTS):
            found += jnp.where(code[k] == p, k, 0)
        sslot[p] = found & 15
        return 0
    lax.fori_loop(0, SLOTS, places, 0)

    inputs[0].wait()
    for i in range(SLOTS):
        s, j = divmod(i, 8)
        value = modes_ref[:, s, LANES * j : LANES * (j + 1)]
        gown[i, 0:MODES, :] = value
        gall[i, 0:MODES, :] = value
    for p in range(SLOTS):
        gsend[p] = gown[sslot[p]]

    lane8 = lax.broadcasted_iota(jnp.int32, (8, LANES), 1)
    lane = lax.broadcasted_iota(jnp.int32, (CASES, LANES), 1)
    low = lane8 < 64

    def pack(x):
        return jnp.where(low, x[0:8], pltpu.roll(x[8:16], 64, 1))

    def unpack(ref):
        out = []
        for j in range(8):
            left, right = ref[2 * j], ref[2 * j + 1]
            up = jnp.where(low, left, pltpu.roll(right, 64, 1))
            down = jnp.where(low, pltpu.roll(left, 64, 1), right)
            out.append(jnp.concatenate([up, down], axis=0))
        return jnp.concatenate(out, axis=1)

    crpad[...] = jnp.zeros_like(crpad)
    inputs[1].wait()
    crpad[:, 0:48] = crhs_ref[...]
    place = pack(crpad[...])
    for i in range(SLOTS):
        place = jnp.where(lane8 == 48 + i, psub[i], place)
    for s in range(2):
        place = jnp.where(lane8 == 112 + s, cluster_ref[s].astype(F32), place)
    crall[mem] = place

    inputs[2].wait()
    parts = split3(qinv_ref[...])
    for t in range(3):
        qs[48 * t : 48 * (t + 1), :] = parts[t]
    qf[...] = jnp.zeros_like(qf)
    for m in range(16):
        qf[0:48, 64 * m : 64 * m + 48] = qinv_ref[:, 48 * m : 48 * (m + 1)]
    for j in range(8):
        cut = slice(LANES * j, LANES * (j + 1))
        parts = split3(qf[:, cut])
        for t in range(3):
            qp[t, :, cut] = parts[t]
    wtf[...] = jnp.zeros_like(wtf)
    ball[...] = jnp.zeros_like(ball)
    for i in range(SLOTS):
        s = i // 8
        wtf[96 + 6 * s : 102 + 6 * s, LANES * i : LANES * (i + 1)] = gown[i, 0:MODES, :]

    pl.semaphore_wait(bar, n_mem + n_rep - 2)

    pending = []
    scatter(lambda peer: crall.at[mem], crall, 0, "mem", mem, n_mem)
    exchange_start(gsend, gall, 1)

    def lanes_of(values, i):
        return values[:, LANES * i : LANES * (i + 1)]

    def schur(src):
        out = []
        for s in range(2):
            flat = jnp.concatenate(
                [src[8 * s + j].astype(BF) for j in range(8)], axis=1
            )
            out.append(mm(flat, kbuf[s]))
        return out

    def lane_sum(x):
        return jnp.sum(x, axis=1, keepdims=True)

    def reduce_start(step, scalars):
        t = (tall0, tall1, tall2)[step]
        e = eb.at[step]
        base = 6 + 4 * step
        flat = jnp.concatenate([town[step, i] for i in range(SLOTS)], axis=1)
        own = dot3(flat, (wt[0], wt[1], wt[2]), nt=True)
        extra = jnp.zeros((8, LANES), F32)
        for k, value in enumerate(scalars):
            value = lane_sum(value)
            extra = jnp.where(lane8 == 48 + k, value[0:8], extra)
            extra = jnp.where(lane8 == 112 + k, value[8:16], extra)
        for part, first, last in ((far, 1, 9), (1 - far, 9, 16)):
            cut = pl.ds(pl.multiple_of(512 * part, 512), 512)
            dense = dot_exact(own, sc[:, cut])
            for j in range(4):
                tile = lanes_of(dense, j)
                up, down = tile[0:8], tile[8:16]
                e[8 * part + 2 * j] = pack(tile) + extra
                e[8 * part + 2 * j + 1] = (
                    jnp.where(low, pltpu.roll(up, 64, 1), down) + extra
                )
            scatter(
                lambda peer: e.at[peer], rs.at[step], base, "mem", mem, n_mem, first, last
            )
        rs[step, mem] = e[mem]
        for p in range(SLOTS):
            tsend[step, p] = town[step, sslot[p]]
        for i in range(SLOTS):
            t[i] = town[step, i]
        pending.append(finish(rs.at[step], base, "mem", mem, n_mem))
        ra[step, rep] = total16(rs, step)
        scatter(lambda peer: ra.at[step, rep], ra.at[step], base + 2, "rep", rep, n_rep)
        exchange_start(tsend.at[step], t, base + 1)
        pending.append(finish(ra.at[step], base + 2, "rep", rep, n_rep))
        tile = total16(ra, step)
        mine = jnp.concatenate([tile, pltpu.roll(tile, 64, 1)], axis=0)
        y = yall.at[step]
        out = ysend.at[step]
        for part, first, last in ((far, 1, 9), (1 - far, 9, 16)):
            cut = pl.ds(pl.multiple_of(1024 * part, 1024), 1024)
            product = dot3(mine, (ball[0, :, cut], ball[1, :, cut], ball[2, :, cut]))
            for m in range(8):
                out[8 * part + m] = lanes_of(product, m)
            scatter(
                lambda peer: out.at[peer], y, base + 3, "mem", mem, n_mem, first, last
            )
        y[mem] = out[mem]
        pending.append(exchange_wait(tsend.at[step], t, base + 1))
        image = [t[i] - t[pos[i]] for i in range(SLOTS)]
        pending.append(finish(y, base + 3, "mem", mem, n_mem))
        z = dot3(total16(yall, step), (wt[0], wt[1], wt[2]))
        sums = [
            jnp.concatenate([mine[0:8, k : k + 1], mine[8:16, k : k + 1]], axis=0)
            for k in (48, 49)
        ]
        return [image[i] - lanes_of(z, i) for i in range(SLOTS)], sums

    pending.append(finish(crall, 0, "mem", mem, n_mem))
    y_slice = dot3(unpack(crall), (qp[0], qp[1], qp[2]), nt=True)
    start[mem] = pack(y_slice)
    scatter(lambda peer: start.at[mem], start, 2, "mem", mem, n_mem)
    heads = jnp.concatenate([crall[m][0:1] for m in range(16)], axis=0)
    source = lax.broadcasted_iota(jnp.int32, (LANES, LANES), 0)
    wanted = 48 + ((lax.broadcasted_iota(jnp.int32, (LANES, LANES), 1) * 43) >> 8)
    widen = jnp.where(source == wanted, 1.0, 0.0).astype(BF)
    rows = mm(heads.astype(BF), widen)
    member = 2 * lax.broadcasted_iota(jnp.int32, (16, LANES), 0).astype(F32)
    for s in range(2):
        own_lane = ((lane * 43) >> 8) == SLOTS + s
        rows = jnp.where(own_lane, member + float(s), rows)
    cluster = jnp.full((16, LANES), -100.0, F32)
    for m in range(16):
        for s in range(2):
            k = 112 + s
            number = jnp.broadcast_to(heads[m : m + 1, k : k + 1], (16, LANES))
            cluster = jnp.where(rows == 2.0 * m + s, number, cluster)
    entry16 = (lane * 43) >> 8
    mode16 = (lane - MODES * entry16).astype(F32)
    index = jnp.where(entry16 < 18, 6.0 * cluster + mode16, -100.0)
    for m in range(16):
        index_ref[m] = index[m : m + 1]
    column = jnp.transpose(jnp.broadcast_to(index_ref[mem], (LANES, LANES)))
    in_half = lax.broadcasted_iota(jnp.int32, (LANES, LANES), 1)
    whole = jnp.where(
        (in_half & 63) < 48, 48 * (in_half >> 6) + (in_half & 63), -1
    ).astype(F32)
    for j in range(8):
        hit = jnp.logical_and(whole >= 0.0, whole + 96.0 * j == column)
        sc[:, LANES * j : LANES * (j + 1)] = jnp.where(hit, 1.0, 0.0).astype(BF)

    pending.append(exchange_wait(gsend, gall, 1))
    for i in range(SLOTS):
        got = gall[pos[i]]
        wtf[6 * i : 6 * i + 6, LANES * i : LANES * (i + 1)] = -got[0:MODES]
    for i in range(SLOTS):
        cut = slice(LANES * i, LANES * (i + 1))
        parts = split3(wtf[:, cut])
        for t in range(3):
            wt[t, :, cut] = parts[t]

    number = lax.broadcasted_iota(jnp.int32, (768, LANES), 0).astype(F32)
    for m in range(16):
        hit = number == jnp.broadcast_to(index_ref[m], (768, LANES))
        chosen = mm(qs[...], jnp.where(hit, 1.0, 0.0).astype(BF))
        for t in range(3):
            ball[t, 0:48, LANES * m : LANES * (m + 1)] = (
                chosen[48 * t : 48 * (t + 1)].astype(BF)
            )

    pending.append(finish(start, 2, "mem", mem, n_mem))
    picked = dot_exact(unpack(start), sc[...], nt=True)
    z = dot3(picked, (wt[0], wt[1], wt[2]))
    for i in range(SLOTS):
        lam[i] = lanes_of(z, i)
    inputs[3].wait()
    kcopy.wait()
    zero = jnp.zeros((CASES, LANES), F32)
    terms = schur(lam)
    for i in range(SLOTS):
        s, j = divmod(i, 8)
        cut = slice(LANES * j, LANES * (j + 1))
        town[0, i] = rhs_ref[:, s, cut] - terms[s][:, cut]
    projected, _ = reduce_start(0, ())
    square = zero
    for i in range(SLOTS):
        p0[i] = projected[i]
        square = square + projected[i] * projected[i]

    terms = schur(p0)
    curve = zero
    for i in range(SLOTS):
        s, j = divmod(i, 8)
        value = terms[s][:, LANES * j : LANES * (j + 1)]
        town[1, i] = value
        curve = curve + value * p0[i]
    image, (curvature, norm) = reduce_start(1, (curve, square))
    norm = 0.5 * norm
    alpha = norm / curvature
    square = zero
    for i in range(SLOTS):
        value = p0[i] - alpha * image[i]
        p1[i] = value
        square = square + value * value
    diagonal = lax.broadcasted_iota(jnp.int32, (CASES, LANES), 0) == lane
    as_row = jnp.sum(
        jnp.where(diagonal, lane_sum(square), 0.0), axis=0, keepdims=True
    )
    tm[mem] = as_row
    scatter(lambda peer: tm.at[mem], tm, 18, "mem", mem, n_mem)
    for i in range(SLOTS):
        lam[i] = lam[i] + alpha * p0[i]
    pending.append(finish(tm, 18, "mem", mem, n_mem))
    tr[rep] = total16(tm)
    scatter(lambda peer: tr.at[rep], tr, 19, "rep", rep, n_rep)
    pending.append(finish(tr, 19, "rep", rep, n_rep))
    fresh = 0.5 * lane_sum(
        jnp.where(diagonal, jnp.broadcast_to(total16(tr), (CASES, LANES)), 0.0)
    )
    beta = fresh / norm
    for i in range(SLOTS):
        d1[i] = p1[i] + beta * p0[i]

    terms = schur(d1)
    curve = zero
    for i in range(SLOTS):
        s, j = divmod(i, 8)
        value = terms[s][:, LANES * j : LANES * (j + 1)]
        town[2, i] = value
        curve = curve + value * d1[i]
    image, (curvature, _) = reduce_start(2, (curve,))
    alpha = fresh / curvature
    for i in range(SLOTS):
        s, j = divmod(i, 8)
        cut = slice(LANES * j, LANES * (j + 1))
        outs[0, :, s, cut] = sgn[i] * (lam[i] + alpha * d1[i])
        outs[1, :, s, cut] = sgn[i] * (p1[i] - alpha * image[i])

    for copy in pending:
        copy.wait_send()


def local(
    n_rep, n_mem,
    schur_blocks, rigid_modes, coarse_inverse, coarse_rhs, subdomain_rhs, partner, cluster_of,
):
    vmem = pl.BlockSpec(memory_space=pltpu.VMEM)
    smem = pl.BlockSpec(memory_space=pltpu.SMEM)
    out = jax.ShapeDtypeStruct((2, CASES, 2, 1024), F32)
    tile = (CASES, LANES)
    found = pl.pallas_call(
        functools.partial(kernel, n_rep, n_mem),
        out_shape=out,
        in_specs=[smem, smem] + [pl.BlockSpec(memory_space=pl.ANY)] * 5,
        out_specs=vmem,
        scratch_shapes=[
            pltpu.VMEM((MODES, 2, 1024), F32),
            pltpu.VMEM((48, 768), F32),
            pltpu.VMEM((CASES, 48), F32),
            pltpu.VMEM((CASES, 2, 1024), F32),
            pltpu.VMEM((2, 1024, 1024), BF),
            pltpu.VMEM((LANES, 2048), F32),
            pltpu.VMEM((3, LANES, 2048), BF),
            pltpu.VMEM((LANES, 1024), F32),
            pltpu.VMEM((3, LANES, 1024), BF),
            pltpu.VMEM((144, 768), BF),
            pltpu.VMEM((3, LANES, 2048), BF),
            pltpu.VMEM((LANES, 1024), BF),
            pltpu.VMEM((2 * SLOTS, MODES, LANES), F32),
            pltpu.VMEM((SLOTS, MODES, LANES), F32),
            pltpu.VMEM((SLOTS, MODES, LANES), F32),
            pltpu.VMEM((2 * SLOTS, *tile), F32),
            pltpu.VMEM((2 * SLOTS, *tile), F32),
            pltpu.VMEM((2 * SLOTS, *tile), F32),
            pltpu.VMEM((STEPS, SLOTS, *tile), F32),
            pltpu.VMEM((STEPS, SLOTS, *tile), F32),
            pltpu.VMEM(tile, F32),
            pltpu.VMEM((16, 8, LANES), F32),
            pltpu.VMEM((16, 8, LANES), F32),
            pltpu.VMEM((16, 1, LANES), F32),
            pltpu.VMEM((STEPS, 16, *tile), F32),
            pltpu.VMEM((STEPS, 16, *tile), F32),
            pltpu.VMEM((STEPS, 16, 8, LANES), F32),
            pltpu.VMEM((STEPS, 16, 8, LANES), F32),
            pltpu.VMEM((STEPS, 16, 8, LANES), F32),
            pltpu.VMEM((16, 1, LANES), F32),
            pltpu.VMEM((16, 1, LANES), F32),
            pltpu.VMEM((SLOTS, *tile), F32),
            pltpu.VMEM((SLOTS, *tile), F32),
            pltpu.VMEM((SLOTS, *tile), F32),
            pltpu.VMEM((SLOTS, *tile), F32),
            pltpu.SMEM((SLOTS,), jnp.int32),
            pltpu.SMEM((SLOTS,), jnp.int32),
            pltpu.SMEM((SLOTS,), jnp.int32),
            pltpu.SMEM((SLOTS,), jnp.int32),
            pltpu.SMEM((SLOTS,), F32),
            pltpu.SMEM((SLOTS,), F32),
            pltpu.SemaphoreType.DMA((5,)),
            pltpu.SemaphoreType.DMA((20,)),
            pltpu.SemaphoreType.DMA((20,)),
        ],
        compiler_params=pltpu.CompilerParams(
            collective_id=0, has_side_effects=True, vmem_limit_bytes=60 * 1024 * 1024
        ),
    )(
        partner, cluster_of, jnp.swapaxes(rigid_modes, 0, 1), coarse_inverse.T, coarse_rhs, subdomain_rhs,
        schur_blocks,
    )
    return found[0], found[1]


def solution(mesh):
    placed = (
        P(("rep", "mem"), None, None),
        P(("rep", "mem"), None, None),
        P(None, "mem"),
        P(None, "mem"),
        P(None, ("rep", "mem"), None),
        P(("rep", "mem"), None),
        P(("rep", "mem")),
    )
    return jax.shard_map(
        functools.partial(local, mesh.shape["rep"], mesh.shape["mem"]),
        mesh=mesh,
        in_specs=placed,
        out_specs=(P(None, ("rep", "mem"), None), P(None, ("rep", "mem"), None)),
        check_vma=False,
    )
```
